128 devices in a mesh: row: 16 (over x_hi, z, core), col: 8 (over y, x_lo).
Axes of the slice: x: 4 (x_hi: 2, x_lo: 2; x = x_hi * 2 + x_lo), y: 4, z: 4, core: 2. Of those that a mesh axis runs over, the one named last changes fastest.
Arguments:
- samples: bfloat16 [2048, 1024], P('row'), may hold values from -6 to 6
- frequencies: bfloat16 [1024, 16384], P(None, ('row', 'col')), may hold values from -0.375 to 0.375
- phases: bfloat16 [16384], P(('row', 'col')), may hold values from 0 to 6.28125
Outputs:
- gram_matrix: float32 [16384, 16384], P('row', 'col')
The draws below stay inside these ranges and needn't reach their ends.
All inputs are finite; a program needn't handle non-finite values.
Results may differ from the reference program's by a relative error of at most 0.0014.
Values may be sent and summed in bfloat16 or wider, within the bound.
A program may use at most 64 MiB of HBM per device.

```python
import jax
import jax.numpy as jnp

F = 16384
DIN = 1024
S = 2048
N_ROW = 16
N_COL = 8


def levels(key, dims, cuts, smallest, largest):
    def one(dim, shards_of):
        heights = jax.random.uniform(jax.random.fold_in(jax.random.fold_in(key, 6), dim), (shards_of,), jnp.float32, smallest / len(cuts), largest / len(cuts))
        return jnp.repeat(jnp.exp(heights), dims[dim] // shards_of).reshape((-1,) + (1,) * (len(dims) - dim - 1))

    loudness = one(*cuts[0])
    for cut in cuts[1:]:
        loudness = loudness * one(*cut)
    return loudness


def centred(key, shape, scale, most, shards=(), kind=jnp.bfloat16):
    array = scale * jax.random.normal(key, shape, jnp.float32)
    if shards:
        array = array * levels(key, shape, shards, -0.22, 0.18)
    return jnp.clip(array, -most, most).astype(kind)


def setup_inputs(seed: int = 0) -> dict:
    key_of = jax.random.split(jax.random.key(seed), 4)
    samples = centred(key_of[0], (S, DIN), 1.0, 6.0, ((0, 16),))
    frequencies = centred(key_of[1], (DIN, F), (DIN // 4) ** -0.5, 0.375, ((1, 128),))
    phases = jnp.clip(6.28125 * jax.random.uniform(key_of[2], (F,), jnp.float32) ** levels(key_of[2], (F,), ((0, 128),), -0.2, 0.2), 0.0, 6.28125).astype(jnp.bfloat16)
    return dict(samples=samples, frequencies=frequencies, phases=phases)


def reference(samples, frequencies, phases):
    projected = jnp.dot(samples, frequencies, preferred_element_type=jnp.float32) + phases.astype(jnp.float32)
    features = jnp.cos(projected).astype(jnp.bfloat16)
    sample_count = features.shape[0]
    reordered = features.reshape(sample_count, N_ROW, N_COL, F // (N_ROW * N_COL))
    reordered = reordered.transpose(0, 2, 1, 3).reshape(sample_count, F)
    gram_matrix = jnp.dot(features.T, reordered, preferred_element_type=jnp.float32)
    return gram_matrix * (2.0 / sample_count)
```

```python
import functools

import jax
import jax.numpy as jnp
import numpy as np
from jax import lax
from jax.experimental import pallas as pl
from jax.experimental.pallas import tpu as pltpu
from jax.sharding import PartitionSpec as P

MESH = pl.DeviceIdType.MESH
F32, BF16 = jnp.float32, jnp.bfloat16
MSG = 1040
INV_TWO_PI = np.float32(1.0 / (2.0 * np.pi))
SINE = (6.283164044230108, -41.33714235953727, 81.34076844401463, -70.99342854258839)
LEFT_ORDER = ((0, 0), (1, 0), (0, 1), (0, 3), (1, 1), (1, 3), (0, 2), (1, 2))


def coords():
    row, col = lax.axis_index("row"), lax.axis_index("col")
    return row // 8, (row // 2) % 4, row % 2, col // 2, col % 2


def cosine(acc, phase_turns, scale):
    turns = acc * INV_TWO_PI + phase_turns
    y = 0.25 - jnp.abs(turns - jnp.round(turns))
    u = y * y
    poly = np.float32(SINE[-1] * scale)
    for coeff in SINE[-2::-1]:
        poly = poly * u + np.float32(coeff * scale)
    return (poly * y).astype(BF16)


def features_kernel(scale, samples, freqs, phases, left_out, right_out, sall, rmsg, lmsg, ft, lph, ssem, rsem):
    xh, z, k, y, xl = coords()
    here = lambda xh_, z_, k_, y_, xl_: ((xh_ * 4 + z_) * 2 + k_, y_ * 2 + xl_)
    dz = lambda d: here(xh, (z + d) % 4, k, y, xl)
    dy = lambda d: here(xh, z, k, (y + d) % 4, xl)
    sib = here(xh, z, 1 - k, y, xl)
    across = here(1 - xh, z, k, y, xl)
    mate_a = here(xh, z, k, y, 1 - xl)
    mate_b = here(1 - xh, z, k, y, 1 - xl)

    own = pl.ds(pl.multiple_of(k * 128, 128), 128)

    sall[0, own, :] = samples[...]
    rmsg[0, 0:1024, :] = freqs[...]
    rmsg[0, 1024:MSG, :] = jnp.broadcast_to(phases[...], (16, 128))

    barrier = pltpu.get_barrier_semaphore()
    partners = (dz(1), dz(3), dy(1), dy(3), sib, across, mate_a, mate_b)
    for partner in partners:
        pl.semaphore_signal(barrier, inc=1, device_id=partner, device_id_type=MESH)
    pl.semaphore_wait(barrier, len(partners))

    copies = {}

    def send(name, src, dst, device):
        n = len(copies)
        copy = pltpu.make_async_remote_copy(
            src_ref=src, dst_ref=dst, send_sem=ssem.at[n], recv_sem=rsem.at[n],
            device_id=device, device_id_type=MESH,
        )
        copy.start()
        copies[name] = copy

    def arrive(*names):
        for name in names:
            copies[name].wait_recv()

    def shard(b):
        return sall.at[b, own, :]

    def half(b, h):
        return sall.at[b, pl.ds(pl.multiple_of(k * 128 + h * 64, 64), 64), :]

    def to_sib(b):
        send(f"sib{b}", shard(b), shard(b), sib)

    def to_b(b):
        send(f"b{b}", half(b, 1 - xl), half(4 + b, 1 - xl), mate_b)

    def to_a(b):
        send(f"a{b}", half(4 + b, xl), half(4 + b, xl), mate_a)

    lo, hi = pl.ds(0, 512), pl.ds(512, MSG - 512)

    def ring(tag, buf, base, dev, src=None):
        src = buf.at[base] if src is None else src
        send(f"{tag}{base}+", src, buf.at[base + 3], dev(1))
        send(f"{tag}{base}-", src, buf.at[base + 1], dev(3))

    def ring_forward(tag, buf, base, dev):
        arrive(f"{tag}{base}+")
        send(f"{tag}{base}++", buf.at[base + 3, lo], buf.at[base + 2, lo], dev(1))
        arrive(f"{tag}{base}-")
        send(f"{tag}{base}--", buf.at[base + 1, hi], buf.at[base + 2, hi], dev(3))

    def ring_last(tag, base):
        arrive(f"{tag}{base}++", f"{tag}{base}--")

    def transpose(slot):
        other, steps = LEFT_ORDER[slot]
        src = rmsg.at[0] if slot == 0 else lmsg.at[other * 4 + steps]
        for t in range(8):
            ft[slot * 128:(slot + 1) * 128, t * 128:(t + 1) * 128] = src[t * 128:(t + 1) * 128, :].T
        ph = src[1024:1040, :][0:1, :].astype(F32) * INV_TWO_PI
        lph[slot * 128:(slot + 1) * 128, :] = jnp.broadcast_to(ph, (128, 128)).T

    def left_step(h, b):
        rows = pl.ds(h * 512, 512)
        acc = lax.dot_general(ft[rows, :], sall[b], (((1,), (1,)), ((), ())), preferred_element_type=F32)
        ph = lph[rows, :]
        left_out[rows, pl.ds(pl.multiple_of(b * 256, 256), 256)] = cosine(acc, jnp.concatenate([ph, ph], axis=1), scale)

    def column(d, steps):
        return ((xh + d) % 2 * 4 + (z + steps) % 4) * 2 + k

    def right_step(p, q):
        pair = (rmsg.at[p], rmsg.at[4 + p])
        weights = jnp.concatenate([m[0:1024, :] for m in pair], axis=1)
        ph = jnp.concatenate([m[1024:1040, :][0:1, :] for m in pair], axis=1).astype(F32) * INV_TWO_PI
        block = sall[q * 4:q * 4 + 4].reshape(1024, 1024)
        acc = lax.dot_general(block, weights, (((1,), (0,)), ((), ())), preferred_element_type=F32)
        out = cosine(acc, ph, 1.0)
        for d in range(2):
            right_out[column(d, p), q * 1024:(q + 1) * 1024, :] = out[:, d * 128:(d + 1) * 128]

    def share(p):
        for d in range(2):
            ref = right_out.at[column(d, p)]
            send(f"r{p}{d}", ref, ref, sib)

    send("s+", shard(0), shard(3), dz(1))
    send("s-", shard(0), shard(1), dz(3))
    to_b(0)
    to_sib(0)
    send("la", rmsg.at[0], lmsg.at[4], mate_a)
    ring("l", lmsg, 0, dy, rmsg.at[0])
    send("rx", rmsg.at[0], rmsg.at[4], across)
    transpose(0)

    arrive("s+")
    send("s++", sall.at[3, pl.ds(pl.multiple_of(k * 128, 128), 64), :], sall.at[2, pl.ds(pl.multiple_of(k * 128, 128), 64), :], dz(1))
    to_b(3)
    to_sib(3)
    arrive("s-")
    send("s--", sall.at[1, pl.ds(pl.multiple_of(k * 128 + 64, 64), 64), :], sall.at[2, pl.ds(pl.multiple_of(k * 128 + 64, 64), 64), :], dz(3))
    to_b(1)
    to_sib(1)
    ring("r", rmsg, 0, dz)

    arrive("b0")
    to_a(0)
    arrive("la")
    ring("l", lmsg, 4, dy)
    transpose(1)
    ring_forward("l", lmsg, 0, dy)
    transpose(2)
    transpose(3)
    arrive("sib0")
    left_step(0, 0)
    arrive("rx")
    ring("r", rmsg, 4, dz)
    arrive("s++", "s--")
    to_b(2)
    to_sib(2)
    arrive("sib3")
    left_step(0, 3)
    arrive("b3")
    to_a(3)
    arrive("b1")
    to_a(1)
    arrive("sib1")
    left_step(0, 1)
    arrive("a0")
    to_sib(4)
    ring_forward("l", lmsg, 4, dy)
    transpose(4)
    transpose(5)
    arrive("sib2")
    left_step(0, 2)
    arrive("b2")
    to_a(2)
    arrive("a3")
    to_sib(7)
    arrive("a1")
    to_sib(5)
    ring_forward("r", rmsg, 0, dz)
    right_step(0, 0)
    ring_last("l", 0)
    transpose(6)
    arrive("a2")
    to_sib(6)
    ring_last("l", 4)
    transpose(7)
    ring_forward("r", rmsg, 4, dz)

    def near(b, carry):
        left_step(1, b)
        return carry

    lax.fori_loop(0, 4, near, 0)
    arrive("sib4", "sib5", "sib6", "sib7")

    def far(b, carry):
        left_step(0, b)
        left_step(1, b)
        return carry

    lax.fori_loop(4, 8, far, 0)
    right_step(0, 1)
    share(0)
    for p in (1, 3, 2):
        if p == 2:
            ring_last("r", 0)
            ring_last("r", 4)
        right_step(p, 0)
        right_step(p, 1)
        share(p)
    for p in range(4):
        arrive(f"r{p}0", f"r{p}1")
    for copy in copies.values():
        copy.wait_send()


def gram_kernel(left, right, out):
    xh, z, k, y, xl = coords()
    weights = jnp.concatenate([right[0], right[1]], axis=1)
    for slot, (other, steps) in enumerate(LEFT_ORDER):
        block = (y + steps) % 4 * 2 + (xl + other) % 2
        acc = jnp.dot(left[slot * 128:(slot + 1) * 128, :], weights, preferred_element_type=F32)
        out[pl.ds(pl.multiple_of(block * 128, 128), 128), :] = acc


def body(samples, frequencies, phases):
    vmem = pl.BlockSpec(memory_space=pltpu.VMEM)
    total = samples.shape[0] * lax.axis_size("row")
    left, right = pl.pallas_call(
        functools.partial(features_kernel, 2.0 / total),
        out_shape=(jax.ShapeDtypeStruct((1024, 2048), BF16), jax.ShapeDtypeStruct((16, 2048, 128), BF16)),
        in_specs=[vmem] * 3,
        out_specs=(vmem, vmem),
        scratch_shapes=[
            pltpu.VMEM((8, 256, 1024), BF16),
            pltpu.VMEM((8, MSG, 128), BF16),
            pltpu.VMEM((8, MSG, 128), BF16),
            pltpu.VMEM((1024, 1024), BF16),
            pltpu.VMEM((1024, 128), F32),
            pltpu.SemaphoreType.DMA((56,)),
            pltpu.SemaphoreType.DMA((56,)),
        ],
        compiler_params=pltpu.CompilerParams(
            collective_id=0, has_side_effects=True, vmem_limit_bytes=40 << 20
        ),
        name="features",
    )(samples, frequencies, phases.reshape(1, 128))
    return pl.pallas_call(
        gram_kernel,
        grid=(8,),
        out_shape=jax.ShapeDtypeStruct((1024, 2048), F32),
        in_specs=[
            pl.BlockSpec((1024, 2048), lambda j: (0, 0)),
            pl.BlockSpec((2, 2048, 128), lambda j: (j, 0, 0)),
        ],
        out_specs=pl.BlockSpec((1024, 256), lambda j: (0, j)),
        compiler_params=pltpu.CompilerParams(vmem_limit_bytes=40 << 20),
        name="gram",
    )(left, right)


def solution(mesh):
    in_specs = (P("row", None), P(None, ("row", "col")), P(("row", "col")))
    out_specs = P("row", "col")
    return jax.shard_map(body, mesh=mesh, in_specs=in_specs, out_specs=out_specs, check_vma=False)
```

```python
import functools

import jax
import jax.numpy as jnp
import numpy as np
from jax import lax
from jax.experimental import pallas as pl
from jax.experimental.pallas import tpu as pltpu
from jax.sharding import PartitionSpec as P

MESH = pl.DeviceIdType.MESH
F32, BF16 = jnp.float32, jnp.bfloat16
MSG = 1040
INV_TWO_PI = np.float32(1.0 / (2.0 * np.pi))
SINE = (6.283164044230108, -41.33714235953727, 81.34076844401463, -70.99342854258839)
PAIRS = ((0, 4), (1, 3), (2, 7), (5, 6))
STEPS = (
    "LAs", "F0s", "L0s", "S0", "l0f+", "l0f-", "S-", "RXlo", "T0", "S+", "RXhi", "l0n", "SB0",
    "N3b", "N1b", "R0s", "T3", "LA", "N2s", "F0", "N1s", "T2", "R4lo", "N2b", "N3s", "T1", "La2",
    "l4f-", "R4hi", "La1", "La0", "r0f+", "r0f-", "l4f+", "A3", "P00", "l0l", "La3", "l4n", "r0n",
    "P10", "A1", "La4", "T6", "T4", "T5", "l4l", "T7", "SB7", "Lb1", "Lb3", "r4f+", "A2", "L7",
    "r4f-", "Lb0", "SB5", "Lb4", "Lb2", "r4n", "L5", "r0l", "SB6", "P20", "P21", "L6", "P11", "P01",
    "Go0", "r4l", "SH1", "SH0", "SH2", "P30", "Go2", "P31", "SH3", "Go1", "Gs0", "Gs1", "Gs2",
)
LEFT_ORDER = ((0, 0), (1, 0), (0, 1), (0, 3), (1, 1), (1, 3), (0, 2), (1, 2))


def coords():
    row, col = lax.axis_index("row"), lax.axis_index("col")
    return row // 8, (row // 2) % 4, row % 2, col // 2, col % 2


def cosine(acc, phase_turns, scale):
    turns = acc * INV_TWO_PI + phase_turns
    y = 0.25 - jnp.abs(turns - jnp.round(turns))
    u = y * y
    poly = np.float32(SINE[-1] * scale)
    for coeff in SINE[-2::-1]:
        poly = poly * u + np.float32(coeff * scale)
    return (poly * y).astype(BF16)


def column(xh, z, k, slot):
    return ((xh + slot // 4) % 2 * 4 + (z + slot) % 4) * 2 + k


def gram_pair(left, right, first, second, store):
    weights = jnp.concatenate([right[first], right[second]], axis=1)
    for m in range(4):
        rows = slice(m * 256, (m + 1) * 256)
        store(rows, jnp.dot(left[rows, :], weights, preferred_element_type=F32))


def features_kernel(scale, samples, freqs, phases, left_out, right_out, gram_out, sall, rmsg, lmsg, ft, lph, own_ph, lsem, ssem, rsem):
    xh, z, k, y, xl = coords()
    here = lambda xh_, z_, k_, y_, xl_: ((xh_ * 4 + z_) * 2 + k_, y_ * 2 + xl_)
    dz = lambda d: here(xh, (z + d) % 4, k, y, xl)
    dy = lambda d: here(xh, z, k, (y + d) % 4, xl)
    sib = here(xh, z, 1 - k, y, xl)
    across = here(1 - xh, z, k, y, xl)
    mate_a = here(xh, z, k, y, 1 - xl)
    mate_b = here(1 - xh, z, k, y, 1 - xl)

    def part(start, size):
        return pl.ds(pl.multiple_of(k * 128 + start, 64), size)

    loads = [
        pltpu.make_async_copy(samples, sall.at[0, part(0, 128), :], lsem.at[0]),
        pltpu.make_async_copy(freqs, rmsg.at[0, 0:1024, :], lsem.at[1]),
        pltpu.make_async_copy(phases, own_ph, lsem.at[2]),
    ]
    for load in loads:
        load.start()

    barrier = pltpu.get_barrier_semaphore()
    partners = (dz(1), dz(3), dy(1), dy(3), sib, across, mate_a, mate_b)
    for partner in partners:
        pl.semaphore_signal(barrier, inc=1, device_id=partner, device_id_type=MESH)
    for load in loads:
        load.wait()
    rmsg[0, 1024:MSG, :] = jnp.broadcast_to(own_ph[...], (16, 128))
    pl.semaphore_wait(barrier, len(partners))

    copies = {}

    def send(name, src, dst, device):
        n = len(copies)
        copy = pltpu.make_async_remote_copy(
            src_ref=src, dst_ref=dst, send_sem=ssem.at[n], recv_sem=rsem.at[n],
            device_id=device, device_id_type=MESH,
        )
        copy.start()
        copies[name] = copy

    arrived = set()

    def arrive(*names):
        for name in names:
            if name not in arrived:
                arrived.add(name)
                copies[name].wait_recv()

    def shard(b):
        return sall.at[b, part(0, 128), :]

    def half(b, h):
        return sall.at[b, part(h * 64, 64), :]

    def to_sib(b):
        send(f"sib{b}", shard(b), shard(b), sib)

    def to_b(b):
        send(f"b{b}", half(b, 1 - xl), half(4 + b, 1 - xl), mate_b)

    def to_a(b):
        send(f"a{b}", half(4 + b, xl), half(4 + b, xl), mate_a)

    lo, hi = pl.ds(0, 512), pl.ds(512, MSG - 512)
    own_lo, own_hi = part(0, 64), part(64, 64)

    def hop(name, source, src, buf, dst, rows, device):
        send(name, source.at[src, rows], buf.at[dst, rows], device)

    def ring(tag, source, src, buf, base, dev):
        hop(f"{tag}+lo", source, src, buf, base + 3, lo, dev(1))
        hop(f"{tag}-hi", source, src, buf, base + 1, hi, dev(3))
        hop(f"{tag}+hi", source, src, buf, base + 3, hi, dev(1))
        hop(f"{tag}-lo", source, src, buf, base + 1, lo, dev(3))

    def transpose(slot):
        other, steps = LEFT_ORDER[slot]
        src = rmsg.at[0] if slot == 0 else lmsg.at[other * 4 + steps]
        for t in range(8):
            ft[slot * 128:(slot + 1) * 128, t * 128:(t + 1) * 128] = src[t * 128:(t + 1) * 128, :].T
        ph = src[1024:1040, :][0:1, :].astype(F32) * INV_TWO_PI
        lph[slot * 128:(slot + 1) * 128, :] = jnp.broadcast_to(ph, (128, 128)).T

    def left_step(first, count, b):
        rows = pl.ds(first * 128, count * 128)
        acc = lax.dot_general(ft[rows, :], sall[b], (((1,), (1,)), ((), ())), preferred_element_type=F32)
        ph = lph[rows, :]
        out = cosine(acc, jnp.concatenate([ph, ph], axis=1), scale)
        for i in range(count):
            other, steps = LEFT_ORDER[first + i]
            block = (y + steps) % 4 * 2 + (xl + other) % 2
            left_out[pl.ds(pl.multiple_of(block * 128, 128), 128), pl.ds(pl.multiple_of(b * 256, 256), 256)] = out[i * 128:(i + 1) * 128, :]

    def right_step(i, q):
        pair = [rmsg.at[slot] for slot in PAIRS[i]]
        weights = jnp.concatenate([m[0:1024, :] for m in pair], axis=1)
        ph = jnp.concatenate([m[1024:1040, :][0:1, :] for m in pair], axis=1).astype(F32) * INV_TWO_PI
        block = sall[q * 4:q * 4 + 4].reshape(1024, 1024)
        acc = lax.dot_general(block, weights, (((1,), (0,)), ((), ())), preferred_element_type=F32)
        out = cosine(acc, ph, 1.0)
        for d, slot in enumerate(PAIRS[i]):
            right_out[column(xh, z, k, slot), q * 1024:(q + 1) * 1024, :] = out[:, d * 128:(d + 1) * 128]

    def share(i):
        for slot in PAIRS[i]:
            ref = right_out.at[column(xh, z, k, slot)]
            send(f"r{slot}", ref, ref, sib)

    def shared(i):
        arrive(*(f"r{slot}" for slot in PAIRS[i]))

    def gram_step(i, core):
        first, second = (column(xh, z, core, slot) for slot in PAIRS[i])

        def store(rows, acc):
            gram_out[first, rows, :] = acc[:, 0:128]
            gram_out[second, rows, :] = acc[:, 128:256]

        gram_pair(left_out, right_out, first, second, store)

    steps = {}

    def step(name, waits, action):
        def go():
            arrive(*waits)
            if action is not None:
                action()

        steps[name] = go

    def samples_out():
        hop("s+lo", sall, 0, sall, 3, own_lo, dz(1))
        hop("s-hi", sall, 0, sall, 1, own_hi, dz(3))
        hop("s+hi", sall, 0, sall, 3, own_hi, dz(1))
        hop("s-lo", sall, 0, sall, 1, own_lo, dz(3))

    step("S0", (), samples_out)
    step("F0s", (), lambda: send("f0", shard(0), shard(4), mate_b))
    step("SB0", (), lambda: to_sib(0))
    step("S+", ("s+lo",), lambda: hop("s++", sall, 3, sall, 2, own_lo, dz(1)))
    step("S-", ("s-hi",), lambda: hop("s--", sall, 1, sall, 2, own_hi, dz(3)))
    for b, ready in ((3, ("s+hi",)), (1, ("s-lo",)), (2, ("s++", "s--"))):
        step(f"N{b}b", ready, functools.partial(to_b, b))
        step(f"N{b}s", ready, functools.partial(to_sib, b))
        step(f"A{b}", (f"b{b}",), functools.partial(to_a, b))
        step(f"SB{4 + b}", (f"a{b}",), functools.partial(to_sib, 4 + b))
    step("F0", ("f0",), lambda: to_sib(4))

    step("LAs", (), lambda: send("la", rmsg.at[0], lmsg.at[4], mate_a))
    step("L0s", (), lambda: ring("l0", rmsg, 0, lmsg, 0, dy))
    step("R0s", (), lambda: ring("r0", rmsg, 0, rmsg, 0, dz))
    step("LA", ("la",), lambda: ring("l4", lmsg, 4, lmsg, 4, dy))
    step("RXlo", (), lambda: hop("rxlo", rmsg, 0, rmsg, 4, lo, across))
    step("RXhi", (), lambda: hop("rxhi", rmsg, 0, rmsg, 4, hi, across))

    def partner_lo():
        hop("r4+lo", rmsg, 4, rmsg, 7, lo, dz(1))
        hop("r4-lo", rmsg, 4, rmsg, 5, lo, dz(3))

    def partner_hi():
        hop("r4-hi", rmsg, 4, rmsg, 5, hi, dz(3))
        hop("r4+hi", rmsg, 4, rmsg, 7, hi, dz(1))

    step("R4lo", ("rxlo",), partner_lo)
    step("R4hi", ("rxhi",), partner_hi)
    for tag, buf, base, dev in (("l0", lmsg, 0, dy), ("l4", lmsg, 4, dy), ("r0", rmsg, 0, dz), ("r4", rmsg, 4, dz)):
        step(f"{tag}f+", (f"{tag}+lo",), functools.partial(hop, f"{tag}++", buf, base + 3, buf, base + 2, lo, dev(1)))
        step(f"{tag}f-", (f"{tag}-hi",), functools.partial(hop, f"{tag}--", buf, base + 1, buf, base + 2, hi, dev(3)))
        step(f"{tag}n", (f"{tag}+hi", f"{tag}-lo"), None)
        step(f"{tag}l", (f"{tag}++", f"{tag}--"), None)

    for i in range(8):
        step(f"T{i}", (), functools.partial(transpose, i))
    for b in range(8):
        step(f"La{b}", (f"sib{b}",), functools.partial(left_step, 0, 4, b))
        step(f"Lb{b}", (f"sib{b}",), functools.partial(left_step, 4, 4, b))
        step(f"L{b}", (f"sib{b}",), functools.partial(left_step, 0, 8, b))
    for i in range(4):
        for q in range(2):
            step(f"P{i}{q}", tuple(f"sib{b}" for b in range(q * 4, q * 4 + 4)), functools.partial(right_step, i, q))
        step(f"SH{i}", (), functools.partial(share, i))
        step(f"Go{i}", (), functools.partial(gram_step, i, k))
        step(f"Gs{i}", tuple(f"r{slot}" for slot in PAIRS[i]), functools.partial(gram_step, i, 1 - k))
    for name in STEPS:
        steps[name]()
    shared(3)
    for copy in copies.values():
        copy.wait_send()


def gram_kernel(left, right, gram, out, last, sems):
    xh, z, k, y, xl = coords()
    copies = []

    def write(src, col, rows):
        n = len(copies)
        copy = pltpu.make_async_copy(
            src, out.at[rows, pl.ds(pl.multiple_of(col * 128, 128), 128)], sems.at[n]
        )
        copy.start()
        copies.append(copy)

    for pair in PAIRS[:-1]:
        for core in range(2):
            for slot in pair:
                col = column(xh, z, core, slot)
                write(gram.at[col], col, slice(0, 1024))
    for core in range(2):
        cols = [column(xh, z, core, slot) for slot in PAIRS[-1]]

        def store(rows, acc):
            for d in range(2):
                last[core * 2 + d, rows, :] = acc[:, d * 128:(d + 1) * 128]
                write(last.at[core * 2 + d, rows, :], cols[d], rows)

        gram_pair(left, right, cols[0], cols[1], store)
    for copy in copies:
        copy.wait()


def body(samples, frequencies, phases):
    vmem = pl.BlockSpec(memory_space=pltpu.VMEM)
    hbm = pl.BlockSpec(memory_space=pltpu.HBM)
    total = samples.shape[0] * lax.axis_size("row")
    left, right, gram = pl.pallas_call(
        functools.partial(features_kernel, 2.0 / total),
        out_shape=(
            jax.ShapeDtypeStruct((1024, 2048), BF16),
            jax.ShapeDtypeStruct((16, 2048, 128), BF16),
            jax.ShapeDtypeStruct((16, 1024, 128), F32),
        ),
        in_specs=[hbm] * 3,
        out_specs=(vmem, vmem, vmem),
        scratch_shapes=[
            pltpu.VMEM((8, 256, 1024), BF16),
            pltpu.VMEM((8, MSG, 128), BF16),
            pltpu.VMEM((8, MSG, 128), BF16),
            pltpu.VMEM((1024, 1024), BF16),
            pltpu.VMEM((1024, 128), F32),
            pltpu.VMEM((1, 128), BF16),
            pltpu.SemaphoreType.DMA((3,)),
            pltpu.SemaphoreType.DMA((64,)),
            pltpu.SemaphoreType.DMA((64,)),
        ],
        compiler_params=pltpu.CompilerParams(
            collective_id=0, has_side_effects=True, vmem_limit_bytes=32 << 20
        ),
        name="features",
    )(*(pltpu.with_memory_space_constraint(v, pltpu.HBM) for v in (samples, frequencies, phases.reshape(1, 128))))
    return pl.pallas_call(
        gram_kernel,
        out_shape=jax.ShapeDtypeStruct((1024, 2048), F32),
        in_specs=[vmem] * 3,
        out_specs=hbm,
        scratch_shapes=[pltpu.VMEM((4, 1024, 128), F32), pltpu.SemaphoreType.DMA((28,))],
        compiler_params=pltpu.CompilerParams(vmem_limit_bytes=32 << 20),
        name="gram",
    )(left, right, gram)


def solution(mesh):
    in_specs = (P("row", None), P(None, ("row", "col")), P(("row", "col")))
    out_specs = P("row", "col")
    return jax.shard_map(body, mesh=mesh, in_specs=in_specs, out_specs=out_specs, check_vma=False)
```

```python
import functools

import jax
import jax.numpy as jnp
import numpy as np
from jax import lax
from jax.experimental import pallas as pl
from jax.experimental.pallas import tpu as pltpu
from jax.sharding import PartitionSpec as P

MESH = pl.DeviceIdType.MESH
F32, BF16 = jnp.float32, jnp.bfloat16
MSG = 1040
INV_TWO_PI = np.float32(1.0 / (2.0 * np.pi))
SINE = (6.283164044230108, -41.33714235953727, 81.34076844401463, -70.99342854258839)
PAIRS = ((0, 3), (1, 2), (4, 7), (5, 6))
STEPS = (
    "LAs", "F0s", "L0s", "S0", "RXhi", "l0f+", "l0f-", "S-", "S+", "N1b", "SB0", "l0n", "LA", "N3s",
    "R0s", "T3", "F0", "T1", "T0", "N2s", "T2", "RXlo", "W3", "La3", "l0l", "N3b", "N1s", "T6",
    "W2", "l4f-", "l4f+", "W0", "W4", "La2", "W1", "r0f+", "A1", "r0f-", "La0", "R4lo", "N2b",
    "l4n", "r0n", "P00", "La1", "La4", "A3", "T5", "T4", "l4l", "R4hi", "T7", "SB5", "Lb0", "Lb2",
    "Lb4", "W5", "A2", "r0l", "Lb3", "Lb5", "P10", "La5", "Lb1", "SB7", "r4f+", "r4f-", "r4n",
    "P20", "SB6", "W7", "L7", "W6", "P01", "P21", "P11", "SH1", "SH0", "r4l", "SH2", "P31", "L6",
    "Go2", "Go0", "Go1", "P30", "V2", "V1", "V0", "SH3", "Gs2", "Gs0", "Gs1",
)
LEFT_ORDER = ((0, 0), (1, 0), (0, 1), (0, 3), (1, 1), (1, 3), (0, 2), (1, 2))


def coords():
    row, col = lax.axis_index("row"), lax.axis_index("col")
    return row // 8, (row // 2) % 4, row % 2, col // 2, col % 2


def cosine(acc, phase_turns, scale):
    turns = acc * INV_TWO_PI + phase_turns
    y = 0.25 - jnp.abs(turns - jnp.round(turns))
    u = y * y
    poly = np.float32(SINE[-1] * scale)
    for coeff in SINE[-2::-1]:
        poly = poly * u + np.float32(coeff * scale)
    return (poly * y).astype(BF16)


def column(xh, z, k, slot):
    return ((xh + slot // 4) % 2 * 4 + (z + slot) % 4) * 2 + k


def gram_pair(left, right, first, second, store):
    weights = jnp.concatenate([right[first], right[second]], axis=1)
    for m in range(4):
        rows = slice(m * 256, (m + 1) * 256)
        store(rows, jnp.dot(left[rows, :], weights, preferred_element_type=F32))


def features_kernel(scale, samples, freqs, phases, left_out, right_out, gram_out, sall, rmsg, lmsg, ft, lph, own_ph, lsem, ssem, rsem):
    xh, z, k, y, xl = coords()
    here = lambda xh_, z_, k_, y_, xl_: ((xh_ * 4 + z_) * 2 + k_, y_ * 2 + xl_)
    dz = lambda d: here(xh, (z + d) % 4, k, y, xl)
    dy = lambda d: here(xh, z, k, (y + d) % 4, xl)
    sib = here(xh, z, 1 - k, y, xl)
    across = here(1 - xh, z, k, y, xl)
    mate_a = here(xh, z, k, y, 1 - xl)
    mate_b = here(1 - xh, z, k, y, 1 - xl)

    def part(start, size):
        return pl.ds(pl.multiple_of(k * 128 + start, 64), size)

    loads = [
        pltpu.make_async_copy(samples, sall.at[0, part(0, 128), :], lsem.at[0]),
        pltpu.make_async_copy(freqs, rmsg.at[0, 0:1024, :], lsem.at[1]),
        pltpu.make_async_copy(phases, own_ph, lsem.at[2]),
    ]
    for load in loads:
        load.start()

    barrier = pltpu.get_barrier_semaphore()
    partners = (dz(1), dz(3), dy(1), dy(3), sib, across, mate_a, mate_b)
    for partner in partners:
        pl.semaphore_signal(barrier, inc=1, device_id=partner, device_id_type=MESH)
    for load in loads:
        load.wait()
    rmsg[0, 1024:MSG, :] = jnp.broadcast_to(own_ph[...], (16, 128))
    pl.semaphore_wait(barrier, len(partners))

    copies = {}

    def send(name, src, dst, device):
        n = len(copies)
        copy = pltpu.make_async_remote_copy(
            src_ref=src, dst_ref=dst, send_sem=ssem.at[n], recv_sem=rsem.at[n],
            device_id=device, device_id_type=MESH,
        )
        copy.start()
        copies[name] = copy

    arrived = set()

    def arrive(*names):
        for name in names:
            if name not in arrived:
                arrived.add(name)
                copies[name].wait_recv()

    def shard(b):
        return sall.at[b, part(0, 128), :]

    def half(b, h):
        return sall.at[b, part(h * 64, 64), :]

    def to_sib(b):
        send(f"sib{b}", shard(b), shard(b), sib)

    def to_b(b):
        send(f"b{b}", half(b, 1 - xl), half(4 + b, 1 - xl), mate_b)

    def to_a(b):
        send(f"a{b}", half(4 + b, xl), half(4 + b, xl), mate_a)

    lo, hi = pl.ds(0, 512), pl.ds(512, MSG - 512)
    own_lo, own_hi = part(0, 64), part(64, 64)

    def hop(name, source, src, buf, dst, rows, device):
        send(name, source.at[src, rows], buf.at[dst, rows], device)

    def ring(tag, source, src, buf, base, dev):
        hop(f"{tag}+lo", source, src, buf, base + 3, lo, dev(1))
        hop(f"{tag}-hi", source, src, buf, base + 1, hi, dev(3))
        hop(f"{tag}+hi", source, src, buf, base + 3, hi, dev(1))
        hop(f"{tag}-lo", source, src, buf, base + 1, lo, dev(3))

    def transpose(slot):
        other, steps = LEFT_ORDER[slot]
        src = rmsg.at[0] if slot == 0 else lmsg.at[other * 4 + steps]
        for t in range(8):
            ft[slot * 128:(slot + 1) * 128, t * 128:(t + 1) * 128] = src[t * 128:(t + 1) * 128, :].T
        ph = src[1024:1040, :][0:1, :].astype(F32) * INV_TWO_PI
        lph[slot * 128:(slot + 1) * 128, :] = jnp.broadcast_to(ph, (128, 128)).T

    def left_step(first, count, b):
        rows = pl.ds(first * 128, count * 128)
        acc = lax.dot_general(ft[rows, :], sall[b], (((1,), (1,)), ((), ())), preferred_element_type=F32)
        ph = lph[rows, :]
        out = cosine(acc, jnp.concatenate([ph, ph], axis=1), scale)
        for i in range(count):
            other, steps = LEFT_ORDER[first + i]
            block = (y + steps) % 4 * 2 + (xl + other) % 2
            left_out[pl.ds(pl.multiple_of(block * 128, 128), 128), pl.ds(pl.multiple_of(b * 256, 256), 256)] = out[i * 128:(i + 1) * 128, :]

    def right_step(i, q):
        pair = [rmsg.at[slot] for slot in PAIRS[i]]
        weights = jnp.concatenate([m[0:1024, :] for m in pair], axis=1)
        ph = jnp.concatenate([m[1024:1040, :][0:1, :] for m in pair], axis=1).astype(F32) * INV_TWO_PI
        block = sall[q * 4:q * 4 + 4].reshape(1024, 1024)
        acc = lax.dot_general(block, weights, (((1,), (0,)), ((), ())), preferred_element_type=F32)
        out = cosine(acc, ph, 1.0)
        for d, slot in enumerate(PAIRS[i]):
            right_out[column(xh, z, k, slot), q * 1024:(q + 1) * 1024, :] = out[:, d * 128:(d + 1) * 128]

    def share(i):
        for slot in PAIRS[i]:
            ref = right_out.at[column(xh, z, k, slot)]
            send(f"r{slot}", ref, ref, sib)

    def shared(i):
        arrive(*(f"r{slot}" for slot in PAIRS[i]))

    def gram_step(i, core):
        first, second = (column(xh, z, core, slot) for slot in PAIRS[i])

        def store(rows, acc):
            gram_out[first, rows, :] = acc[:, 0:128]
            gram_out[second, rows, :] = acc[:, 128:256]

        gram_pair(left_out, right_out, first, second, store)

    steps = {}

    def step(name, waits, action):
        def go():
            arrive(*waits)
            if action is not None:
                action()

        steps[name] = go

    def samples_out():
        hop("s+lo", sall, 0, sall, 3, own_lo, dz(1))
        hop("s-hi", sall, 0, sall, 1, own_hi, dz(3))
        hop("s+hi", sall, 0, sall, 3, own_hi, dz(1))
        hop("s-lo", sall, 0, sall, 1, own_lo, dz(3))

    step("S0", (), samples_out)
    step("F0s", (), lambda: send("f0", shard(0), shard(4), mate_b))
    step("SB0", (), lambda: to_sib(0))
    step("S+", ("s+lo",), lambda: hop("s++", sall, 3, sall, 2, own_lo, dz(1)))
    step("S-", ("s-hi",), lambda: hop("s--", sall, 1, sall, 2, own_hi, dz(3)))
    for b, ready in ((3, ("s+hi",)), (1, ("s-lo",)), (2, ("s++", "s--"))):
        step(f"N{b}b", ready, functools.partial(to_b, b))
        step(f"N{b}s", ready, functools.partial(to_sib, b))
        step(f"A{b}", (f"b{b}",), functools.partial(to_a, b))
        step(f"SB{4 + b}", (f"a{b}",), functools.partial(to_sib, 4 + b))
    step("F0", ("f0",), lambda: to_sib(4))

    step("LAs", (), lambda: send("la", rmsg.at[0], lmsg.at[4], mate_a))
    step("L0s", (), lambda: ring("l0", rmsg, 0, lmsg, 0, dy))
    step("R0s", (), lambda: ring("r0", rmsg, 0, rmsg, 0, dz))
    step("LA", ("la",), lambda: ring("l4", lmsg, 4, lmsg, 4, dy))
    step("RXlo", (), lambda: hop("rxlo", rmsg, 0, rmsg, 4, lo, across))
    step("RXhi", (), lambda: hop("rxhi", rmsg, 0, rmsg, 4, hi, across))

    def partner_lo():
        hop("r4+lo", rmsg, 4, rmsg, 7, lo, dz(1))
        hop("r4-lo", rmsg, 4, rmsg, 5, lo, dz(3))

    def partner_hi():
        hop("r4-hi", rmsg, 4, rmsg, 5, hi, dz(3))
        hop("r4+hi", rmsg, 4, rmsg, 7, hi, dz(1))

    step("R4lo", ("rxlo",), partner_lo)
    step("R4hi", ("rxhi",), partner_hi)
    for tag, buf, base, dev in (("l0", lmsg, 0, dy), ("l4", lmsg, 4, dy), ("r0", rmsg, 0, dz), ("r4", rmsg, 4, dz)):
        step(f"{tag}f+", (f"{tag}+lo",), functools.partial(hop, f"{tag}++", buf, base + 3, buf, base + 2, lo, dev(1)))
        step(f"{tag}f-", (f"{tag}-hi",), functools.partial(hop, f"{tag}--", buf, base + 1, buf, base + 2, hi, dev(3)))
        step(f"{tag}n", (f"{tag}+hi", f"{tag}-lo"), None)
        step(f"{tag}l", (f"{tag}++", f"{tag}--"), None)

    for i in range(8):
        step(f"T{i}", (), functools.partial(transpose, i))
    for b in range(8):
        step(f"W{b}", (f"sib{b}",), None)
        step(f"La{b}", (f"sib{b}",), functools.partial(left_step, 0, 4, b))
        step(f"Lb{b}", (f"sib{b}",), functools.partial(left_step, 4, 4, b))
        step(f"L{b}", (f"sib{b}",), functools.partial(left_step, 0, 8, b))
    for i in range(4):
        for q in range(2):
            step(f"P{i}{q}", tuple(f"sib{b}" for b in range(q * 4, q * 4 + 4)), functools.partial(right_step, i, q))
        step(f"SH{i}", (), functools.partial(share, i))
        step(f"Go{i}", (), functools.partial(gram_step, i, k))
        step(f"Gs{i}", tuple(f"r{slot}" for slot in PAIRS[i]), functools.partial(gram_step, i, 1 - k))
        step(f"V{i}", tuple(f"r{slot}" for slot in PAIRS[i]), None)
    for name in STEPS:
        steps[name]()
    shared(3)
    for copy in copies.values():
        copy.wait_send()


def gram_kernel(left, right, gram, out, last, sems):
    xh, z, k, y, xl = coords()
    copies = []

    def write(src, col, rows):
        n = len(copies)
        copy = pltpu.make_async_copy(
            src, out.at[rows, pl.ds(pl.multiple_of(col * 128, 128), 128)], sems.at[n]
        )
        copy.start()
        copies.append(copy)

    for pair in PAIRS[:-1]:
        for core in range(2):
            for slot in pair:
                col = column(xh, z, core, slot)
                write(gram.at[col], col, slice(0, 1024))
    for core in range(2):
        cols = [column(xh, z, core, slot) for slot in PAIRS[-1]]

        def store(rows, acc):
            for d in range(2):
                last[core * 2 + d, rows, :] = acc[:, d * 128:(d + 1) * 128]
                write(last.at[core * 2 + d, rows, :], cols[d], rows)

        gram_pair(left, right, cols[0], cols[1], store)
    for copy in copies:
        copy.wait()


def body(samples, frequencies, phases):
    vmem = pl.BlockSpec(memory_space=pltpu.VMEM)
    hbm = pl.BlockSpec(memory_space=pltpu.HBM)
    total = samples.shape[0] * lax.axis_size("row")
    left, right, gram = pl.pallas_call(
        functools.partial(features_kernel, 2.0 / total),
        out_shape=(
            jax.ShapeDtypeStruct((1024, 2048), BF16),
            jax.ShapeDtypeStruct((16, 2048, 128), BF16),
            jax.ShapeDtypeStruct((16, 1024, 128), F32),
        ),
        in_specs=[hbm] * 3,
        out_specs=(vmem, vmem, vmem),
        scratch_shapes=[
            pltpu.VMEM((8, 256, 1024), BF16),
            pltpu.VMEM((8, MSG, 128), BF16),
            pltpu.VMEM((8, MSG, 128), BF16),
            pltpu.VMEM((1024, 1024), BF16),
            pltpu.VMEM((1024, 128), F32),
            pltpu.VMEM((1, 128), BF16),
            pltpu.SemaphoreType.DMA((3,)),
            pltpu.SemaphoreType.DMA((64,)),
            pltpu.SemaphoreType.DMA((64,)),
        ],
        compiler_params=pltpu.CompilerParams(
            collective_id=0, has_side_effects=True, vmem_limit_bytes=32 << 20
        ),
        name="features",
    )(*(pltpu.with_memory_space_constraint(v, pltpu.HBM) for v in (samples, frequencies, phases.reshape(1, 128))))
    return pl.pallas_call(
        gram_kernel,
        out_shape=jax.ShapeDtypeStruct((1024, 2048), F32),
        in_specs=[vmem] * 3,
        out_specs=hbm,
        scratch_shapes=[pltpu.VMEM((4, 1024, 128), F32), pltpu.SemaphoreType.DMA((28,))],
        compiler_params=pltpu.CompilerParams(vmem_limit_bytes=32 << 20),
        name="gram",
    )(left, right, gram)


def solution(mesh):
    in_specs = (P("row", None), P(None, ("row", "col")), P(("row", "col")))
    out_specs = P("row", "col")
    return jax.shard_map(body, mesh=mesh, in_specs=in_specs, out_specs=out_specs, check_vma=False)
```

```python
import functools

import jax
import jax.numpy as jnp
import numpy as np
from jax import lax
from jax.experimental import pallas as pl
from jax.experimental.pallas import tpu as pltpu
from jax.sharding import PartitionSpec as P

MESH = pl.DeviceIdType.MESH
F32, BF16 = jnp.float32, jnp.bfloat16
MSG = 1040
INV_TWO_PI = np.float32(1.0 / (2.0 * np.pi))
SINE = (6.283164044230108, -41.33714235953727, 81.34076844401463, -70.99342854258839)
PAIRS = ((0, 3), (1, 2), (4, 7), (5, 6))
STEPS = (
    "LAs", "F0s", "L0s", "S0", "RXhi", "l0f+", "l0f-", "S-", "S+", "N1b", "SB0", "l0n", "LA", "N3s",
    "R0s", "T3", "F0", "T1", "T0", "N2s", "T2", "RXlo", "W3", "La3", "l0l", "N3b", "N1s", "T6",
    "W2", "l4f-", "l4f+", "W0", "W4", "La2", "W1", "r0f+", "A1", "r0f-", "La0", "R4lo", "N2b",
    "l4n", "r0n", "P00", "La1", "La4", "A3", "T5", "T4", "l4l", "R4hi", "T7", "SB5", "Lb0", "Lb2",
    "Lb4", "W5", "A2", "r0l", "Lb3", "Lb5", "P10", "La5", "Lb1", "SB7", "r4f+", "r4f-", "r4n",
    "P20", "SB6", "W7", "L7", "W6", "P01", "P21", "P11", "SH1", "SH0", "r4l", "SH2", "P31", "L6",
    "Go2", "Go0", "Go1", "P30", "V2", "V1", "V0", "SH3", "Gs0", "Gs1",
)
LEFT_ORDER = ((0, 0), (1, 0), (0, 1), (0, 3), (1, 1), (1, 3), (0, 2), (1, 2))


def coords():
    row, col = lax.axis_index("row"), lax.axis_index("col")
    return row // 8, (row // 2) % 4, row % 2, col // 2, col % 2


def cosine(acc, phase_turns, scale):
    turns = acc * INV_TWO_PI + phase_turns
    y = 0.25 - jnp.abs(turns - jnp.round(turns))
    u = y * y
    poly = np.float32(SINE[-1] * scale)
    for coeff in SINE[-2::-1]:
        poly = poly * u + np.float32(coeff * scale)
    return (poly * y).astype(BF16)


def column(xh, z, k, slot):
    return ((xh + slot // 4) % 2 * 4 + (z + slot) % 4) * 2 + k


def gram_pair(left, right, first, second, store):
    weights = jnp.concatenate([right[first], right[second]], axis=1)
    for m in range(4):
        rows = slice(m * 256, (m + 1) * 256)
        store(rows, jnp.dot(left[rows, :], weights, preferred_element_type=F32))


def features_kernel(scale, samples, freqs, phases, left_out, right_out, gram_out, sall, rmsg, lmsg, ft, lph, own_ph, lsem, ssem, rsem):
    xh, z, k, y, xl = coords()
    here = lambda xh_, z_, k_, y_, xl_: ((xh_ * 4 + z_) * 2 + k_, y_ * 2 + xl_)
    dz = lambda d: here(xh, (z + d) % 4, k, y, xl)
    dy = lambda d: here(xh, z, k, (y + d) % 4, xl)
    sib = here(xh, z, 1 - k, y, xl)
    across = here(1 - xh, z, k, y, xl)
    mate_a = here(xh, z, k, y, 1 - xl)
    mate_b = here(1 - xh, z, k, y, 1 - xl)

    def part(start, size):
        return pl.ds(pl.multiple_of(k * 128 + start, 64), size)

    loads = [
        pltpu.make_async_copy(samples, sall.at[0, part(0, 128), :], lsem.at[0]),
        pltpu.make_async_copy(freqs, rmsg.at[0, 0:1024, :], lsem.at[1]),
        pltpu.make_async_copy(phases, own_ph, lsem.at[2]),
    ]
    for load in loads:
        load.start()

    barrier = pltpu.get_barrier_semaphore()
    partners = (dz(1), dz(3), dy(1), dy(3), sib, across, mate_a, mate_b)
    for partner in partners:
        pl.semaphore_signal(barrier, inc=1, device_id=partner, device_id_type=MESH)
    for load in loads:
        load.wait()
    rmsg[0, 1024:MSG, :] = jnp.broadcast_to(own_ph[...], (16, 128))
    pl.semaphore_wait(barrier, len(partners))

    copies = {}

    def send(name, src, dst, device):
        n = len(copies)
        copy = pltpu.make_async_remote_copy(
            src_ref=src, dst_ref=dst, send_sem=ssem.at[n], recv_sem=rsem.at[n],
            device_id=device, device_id_type=MESH,
        )
        copy.start()
        copies[name] = copy

    arrived = set()

    def arrive(*names):
        for name in names:
            if name not in arrived:
                arrived.add(name)
                copies[name].wait_recv()

    def shard(b):
        return sall.at[b, part(0, 128), :]

    def half(b, h):
        return sall.at[b, part(h * 64, 64), :]

    def to_sib(b):
        send(f"sib{b}", shard(b), shard(b), sib)

    def to_b(b):
        send(f"b{b}", half(b, 1 - xl), half(4 + b, 1 - xl), mate_b)

    def to_a(b):
        send(f"a{b}", half(4 + b, xl), half(4 + b, xl), mate_a)

    lo, hi = pl.ds(0, 512), pl.ds(512, MSG - 512)
    own_lo, own_hi = part(0, 64), part(64, 64)

    def hop(name, source, src, buf, dst, rows, device):
        send(name, source.at[src, rows], buf.at[dst, rows], device)

    def ring(tag, source, src, buf, base, dev):
        hop(f"{tag}+lo", source, src, buf, base + 3, lo, dev(1))
        hop(f"{tag}-hi", source, src, buf, base + 1, hi, dev(3))
        hop(f"{tag}+hi", source, src, buf, base + 3, hi, dev(1))
        hop(f"{tag}-lo", source, src, buf, base + 1, lo, dev(3))

    def transpose(slot):
        other, steps = LEFT_ORDER[slot]
        src = rmsg.at[0] if slot == 0 else lmsg.at[other * 4 + steps]
        for t in range(8):
            ft[slot * 128:(slot + 1) * 128, t * 128:(t + 1) * 128] = src[t * 128:(t + 1) * 128, :].T
        ph = src[1024:1040, :][0:1, :].astype(F32) * INV_TWO_PI
        lph[slot * 128:(slot + 1) * 128, :] = jnp.broadcast_to(ph, (128, 128)).T

    def left_step(first, count, b):
        rows = pl.ds(first * 128, count * 128)
        acc = lax.dot_general(ft[rows, :], sall[b], (((1,), (1,)), ((), ())), preferred_element_type=F32)
        ph = lph[rows, :]
        out = cosine(acc, jnp.concatenate([ph, ph], axis=1), scale)
        for i in range(count):
            other, steps = LEFT_ORDER[first + i]
            block = (y + steps) % 4 * 2 + (xl + other) % 2
            left_out[pl.ds(pl.multiple_of(block * 128, 128), 128), pl.ds(pl.multiple_of(b * 256, 256), 256)] = out[i * 128:(i + 1) * 128, :]

    def right_step(i, q):
        pair = [rmsg.at[slot] for slot in PAIRS[i]]
        weights = jnp.concatenate([m[0:1024, :] for m in pair], axis=1)
        ph = jnp.concatenate([m[1024:1040, :][0:1, :] for m in pair], axis=1).astype(F32) * INV_TWO_PI
        block = sall[q * 4:q * 4 + 4].reshape(1024, 1024)
        acc = lax.dot_general(block, weights, (((1,), (0,)), ((), ())), preferred_element_type=F32)
        out = cosine(acc, ph, 1.0)
        for d, slot in enumerate(PAIRS[i]):
            right_out[column(xh, z, k, slot), q * 1024:(q + 1) * 1024, :] = out[:, d * 128:(d + 1) * 128]

    def share(i):
        for slot in PAIRS[i]:
            ref = right_out.at[column(xh, z, k, slot)]
            send(f"r{slot}", ref, ref, sib)

    def shared(i):
        arrive(*(f"r{slot}" for slot in PAIRS[i]))

    def gram_step(i, core):
        first, second = (column(xh, z, core, slot) for slot in PAIRS[i])

        def store(rows, acc):
            gram_out[first, rows, :] = acc[:, 0:128]
            gram_out[second, rows, :] = acc[:, 128:256]

        gram_pair(left_out, right_out, first, second, store)

    steps = {}

    def step(name, waits, action):
        def go():
            arrive(*waits)
            if action is not None:
                action()

        steps[name] = go

    def samples_out():
        hop("s+lo", sall, 0, sall, 3, own_lo, dz(1))
        hop("s-hi", sall, 0, sall, 1, own_hi, dz(3))
        hop("s+hi", sall, 0, sall, 3, own_hi, dz(1))
        hop("s-lo", sall, 0, sall, 1, own_lo, dz(3))

    step("S0", (), samples_out)
    step("F0s", (), lambda: send("f0", shard(0), shard(4), mate_b))
    step("SB0", (), lambda: to_sib(0))
    step("S+", ("s+lo",), lambda: hop("s++", sall, 3, sall, 2, own_lo, dz(1)))
    step("S-", ("s-hi",), lambda: hop("s--", sall, 1, sall, 2, own_hi, dz(3)))
    for b, ready in ((3, ("s+hi",)), (1, ("s-lo",)), (2, ("s++", "s--"))):
        step(f"N{b}b", ready, functools.partial(to_b, b))
        step(f"N{b}s", ready, functools.partial(to_sib, b))
        step(f"A{b}", (f"b{b}",), functools.partial(to_a, b))
        step(f"SB{4 + b}", (f"a{b}",), functools.partial(to_sib, 4 + b))
    step("F0", ("f0",), lambda: to_sib(4))

    step("LAs", (), lambda: send("la", rmsg.at[0], lmsg.at[4], mate_a))
    step("L0s", (), lambda: ring("l0", rmsg, 0, lmsg, 0, dy))
    step("R0s", (), lambda: ring("r0", rmsg, 0, rmsg, 0, dz))
    step("LA", ("la",), lambda: ring("l4", lmsg, 4, lmsg, 4, dy))
    step("RXlo", (), lambda: hop("rxlo", rmsg, 0, rmsg, 4, lo, across))
    step("RXhi", (), lambda: hop("rxhi", rmsg, 0, rmsg, 4, hi, across))

    def partner_lo():
        hop("r4+lo", rmsg, 4, rmsg, 7, lo, dz(1))
        hop("r4-lo", rmsg, 4, rmsg, 5, lo, dz(3))

    def partner_hi():
        hop("r4-hi", rmsg, 4, rmsg, 5, hi, dz(3))
        hop("r4+hi", rmsg, 4, rmsg, 7, hi, dz(1))

    step("R4lo", ("rxlo",), partner_lo)
    step("R4hi", ("rxhi",), partner_hi)
    for tag, buf, base, dev in (("l0", lmsg, 0, dy), ("l4", lmsg, 4, dy), ("r0", rmsg, 0, dz), ("r4", rmsg, 4, dz)):
        step(f"{tag}f+", (f"{tag}+lo",), functools.partial(hop, f"{tag}++", buf, base + 3, buf, base + 2, lo, dev(1)))
        step(f"{tag}f-", (f"{tag}-hi",), functools.partial(hop, f"{tag}--", buf, base + 1, buf, base + 2, hi, dev(3)))
        step(f"{tag}n", (f"{tag}+hi", f"{tag}-lo"), None)
        step(f"{tag}l", (f"{tag}++", f"{tag}--"), None)

    for i in range(8):
        step(f"T{i}", (), functools.partial(transpose, i))
    for b in range(8):
        step(f"W{b}", (f"sib{b}",), None)
        step(f"La{b}", (f"sib{b}",), functools.partial(left_step, 0, 4, b))
        step(f"Lb{b}", (f"sib{b}",), functools.partial(left_step, 4, 4, b))
        step(f"L{b}", (f"sib{b}",), functools.partial(left_step, 0, 8, b))
    for i in range(4):
        for q in range(2):
            step(f"P{i}{q}", tuple(f"sib{b}" for b in range(q * 4, q * 4 + 4)), functools.partial(right_step, i, q))
        step(f"SH{i}", (), functools.partial(share, i))
        step(f"Go{i}", (), functools.partial(gram_step, i, k))
        step(f"Gs{i}", tuple(f"r{slot}" for slot in PAIRS[i]), functools.partial(gram_step, i, 1 - k))
        step(f"V{i}", tuple(f"r{slot}" for slot in PAIRS[i]), None)
    for name in STEPS:
        steps[name]()
    shared(3)
    for copy in copies.values():
        copy.wait_send()


def gram_kernel(left, right, gram, out, last, sems):
    xh, z, k, y, xl = coords()
    copies = []

    def write(src, col, rows):
        n = len(copies)
        copy = pltpu.make_async_copy(
            src, out.at[rows, pl.ds(pl.multiple_of(col * 128, 128), 128)], sems.at[n]
        )
        copy.start()
        copies.append(copy)

    done = [(i, core) for i in (0, 1) for core in (0, 1)] + [(2, k)]
    for i, core in done:
        for slot in PAIRS[i]:
            col = column(xh, z, core, slot)
            write(gram.at[col], col, slice(0, 1024))
    for n, (i, core) in enumerate(((2, 1 - k), (3, 0), (3, 1))):
        cols = [column(xh, z, core, slot) for slot in PAIRS[i]]

        def store(rows, acc):
            for d in range(2):
                last[n * 2 + d, rows, :] = acc[:, d * 128:(d + 1) * 128]
            size = 512 if n == 2 else 1024
            if rows.stop % size == 0:
                ready = slice(rows.stop - size, rows.stop)
                for d in range(2):
                    write(last.at[n * 2 + d, ready, :], cols[d], ready)

        gram_pair(left, right, cols[0], cols[1], store)
    for copy in copies:
        copy.wait()


def body(samples, frequencies, phases):
    vmem = pl.BlockSpec(memory_space=pltpu.VMEM)
    hbm = pl.BlockSpec(memory_space=pltpu.HBM)
    total = samples.shape[0] * lax.axis_size("row")
    left, right, gram = pl.pallas_call(
        functools.partial(features_kernel, 2.0 / total),
        out_shape=(
            jax.ShapeDtypeStruct((1024, 2048), BF16),
            jax.ShapeDtypeStruct((16, 2048, 128), BF16),
            jax.ShapeDtypeStruct((16, 1024, 128), F32),
        ),
        in_specs=[hbm] * 3,
        out_specs=(vmem, vmem, vmem),
        scratch_shapes=[
            pltpu.VMEM((8, 256, 1024), BF16),
            pltpu.VMEM((8, MSG, 128), BF16),
            pltpu.VMEM((8, MSG, 128), BF16),
            pltpu.VMEM((1024, 1024), BF16),
            pltpu.VMEM((1024, 128), F32),
            pltpu.VMEM((1, 128), BF16),
            pltpu.SemaphoreType.DMA((3,)),
            pltpu.SemaphoreType.DMA((64,)),
            pltpu.SemaphoreType.DMA((64,)),
        ],
        compiler_params=pltpu.CompilerParams(
            collective_id=0, has_side_effects=True, vmem_limit_bytes=32 << 20
        ),
        name="features",
    )(*(pltpu.with_memory_space_constraint(v, pltpu.HBM) for v in (samples, frequencies, phases.reshape(1, 128))))
    return pl.pallas_call(
        gram_kernel,
        out_shape=jax.ShapeDtypeStruct((1024, 2048), F32),
        in_specs=[vmem] * 3,
        out_specs=hbm,
        scratch_shapes=[pltpu.VMEM((6, 1024, 128), F32), pltpu.SemaphoreType.DMA((34,))],
        compiler_params=pltpu.CompilerParams(vmem_limit_bytes=32 << 20),
        name="gram",
    )(left, right, gram)


def solution(mesh):
    in_specs = (P("row", None), P(None, ("row", "col")), P(("row", "col")))
    out_specs = P("row", "col")
    return jax.shard_map(body, mesh=mesh, in_specs=in_specs, out_specs=out_specs, check_vma=False)
```
